32 devices in a mesh: pole: 4 (over y, x), grid: 8 (over z, core).
Axes of the slice: x: 2, y: 2, z: 4, core: 2. Of those that a mesh axis runs over, the one named last changes fastest.
Arguments:
- hamiltonian: float32 [2048, 2048], P(('pole', 'grid')), may hold values from -6 to 6, as said below
- margin: float32 [2048, 2048], P(('pole', 'grid')), may hold values from -1 to 1.2, as said below
- pattern: int32 [4, 4], replicated, may hold values 0 or 1
- shift_real: float32 [4], P('pole'), may hold values from -0.5 to 0.5
- shift_imag: float32 [4], P('pole'), may hold values from 0.3 to 3
- residue: float32 [4, 2], P('pole'), may hold values from -4 to 4
Outputs:
- density: float32 [2048, 2048], P(('pole', 'grid'))
The draws below stay inside these ranges and needn't reach their ends.
Inputs may be any that keep to these rules, and one draw needn't show every extreme that they name: `hamiltonian`: symmetric. `margin`: symmetric.
All inputs are finite; a program needn't handle non-finite values.
Results may differ from the reference program's by a relative error of at most 0.0003.
Values sent between devices are 32-bit elements; how exact they have to be, the bound alone decides.
No kernel may reach another device: no remote copies, remote signals or barrier semaphores. Data moves between devices by JAX's collectives and lax.ppermute only.
A program may use at most 320 MiB of HBM per device.

```python
import math
import jax
import jax.numpy as jnp
from jax import lax

SUPER = 256
NC = 2
NR = 4
C = 512
R = 1024
N = 2048
POLES = 4


def draw_hamiltonian(key, part):
    key_off, key_mag, key_sign = jax.random.split(jax.random.fold_in(key, 101), 3)
    spread = jax.random.normal(key_off, (N, N), jnp.float32)
    spread = (spread + spread.T) * (1.4 / math.sqrt(2.0 * N))
    magnitude = jax.random.uniform(key_mag, (N,), jnp.float32, 3.0, 6.0)
    signs = jnp.where(jax.random.bernoulli(key_sign, 0.5, (N,)), 1.0, -1.0)
    eye = jnp.eye(N, dtype=jnp.float32)
    return spread * (1.0 - eye) + jnp.diag(magnitude * signs)


def draw_margin(key, part):
    key_off, key_mag = jax.random.split(jax.random.fold_in(key, 202), 2)
    spread = jax.random.normal(key_off, (N, N), jnp.float32)
    spread = (spread + spread.T) * (0.3 / math.sqrt(2.0 * N))
    spread = jnp.clip(spread, -0.9, 0.9)
    magnitude = jax.random.uniform(key_mag, (N,), jnp.float32, 0.8, 1.2)
    eye = jnp.eye(N, dtype=jnp.float32)
    return spread * (1.0 - eye) + jnp.diag(magnitude)


def touch_ends(drawn, key, smallest, top_value):
    extent = drawn.shape
    spot = [jax.random.randint(jax.random.fold_in(key, axis), (), 0, extent[axis]) for axis in range(len(extent))]
    drawn = drawn.at[tuple(spot)].set(smallest)
    longest = extent.index(max(extent))
    spot[longest] = (spot[longest] + 1) % extent[longest]
    return drawn.at[tuple(spot)].set(top_value)


def block_scale(rng, shape, shards, low, largest):
    loudness = 1.0
    for axis_at, shards_of in shards:
        heights = jax.random.uniform(jax.random.fold_in(jax.random.fold_in(rng, 6), axis_at), (shards_of,), jnp.float32, low / len(shards), largest / len(shards))
        loudness = loudness * jnp.repeat(jnp.exp(heights), shape[axis_at] // shards_of).reshape((-1,) + (1,) * (len(shape) - 1 - axis_at))
    return loudness


def normal_values(rng, shape, scale, most, cuts=(), kind=jnp.bfloat16):
    entries = scale * jax.random.normal(rng, shape, jnp.float32)
    if cuts:
        entries = entries * block_scale(rng, shape, cuts, -0.22, 0.18)
    return jnp.clip(entries, -most, most).astype(kind)


def setup_inputs(seed: int = 0) -> dict:
    keys = jax.random.split(jax.random.key(seed), 7)
    return {
        "hamiltonian": draw_hamiltonian(jax.random.fold_in(keys[6], 71), 0),
        "margin": draw_margin(jax.random.fold_in(keys[6], 71), 0),
        "pattern": touch_ends((jax.random.randint(keys[2], (NR, 2 * NC), 0, 4) < 3).astype(jnp.int32), jax.random.fold_in(keys[2], 1), 0, 1),
        "shift_real": jnp.clip(jax.random.uniform(keys[3], (POLES,), jnp.float32, -0.5, 0.5) * block_scale(keys[3], (POLES,), ((0, 4),), -0.4, 0.0), -0.5, 0.5),
        "shift_imag": jnp.clip(jnp.exp(math.log(3.0) - 2.3025851 * jax.random.uniform(keys[4], (POLES,), jnp.float32) ** block_scale(keys[4], (POLES,), ((0, 4),), -0.2, 0.2)), 0.3, 3.0),
        "residue": normal_values(keys[5], (POLES, 2), 1.0, 4.0, ((0, 4),), jnp.float32),
    }


HIGH = lax.Precision.HIGHEST


def cdot(left, right):
    def mult(a, b):
        return jnp.dot(a, b, precision=HIGH, preferred_element_type=jnp.float32)
    return mult(left[0], right[0]) - mult(left[1], right[1]), mult(left[0], right[1]) + mult(left[1], right[0])


def cmul(left, right):
    return left[0] * right[0] - left[1] * right[1], left[0] * right[1] + left[1] * right[0]


def newton(matrix):
    size = matrix[0].shape[0]
    diag_real = jnp.diagonal(matrix[0])
    diag_imag = jnp.diagonal(matrix[1])
    denom = diag_real * diag_real + diag_imag * diag_imag
    inv_real = diag_real / denom
    inv_imag = -diag_imag / denom
    scaled = cmul((inv_real[:, None], inv_imag[:, None]), matrix)
    scaled = cmul(scaled, (inv_real[None, :], inv_imag[None, :]))
    eye = jnp.eye(size, dtype=jnp.float32)
    start = (2.0 * eye * inv_real[None, :] - scaled[0], 2.0 * eye * inv_imag[None, :] - scaled[1])
    product = cdot(start, matrix)
    product = cdot(product, start)
    return (2.0 * start[0] - product[0], 2.0 * start[1] - product[1])


def build_mask(pattern):
    blocks = jnp.repeat(jnp.repeat(pattern.astype(jnp.float32), SUPER, axis=0), SUPER, axis=1)
    ones_child = jnp.ones((C, C), jnp.float32)
    zero_child = jnp.zeros((C, C), jnp.float32)
    top = jnp.concatenate([ones_child, zero_child, blocks[:, :C].T], axis=1)
    middle = jnp.concatenate([zero_child, ones_child, blocks[:, C:].T], axis=1)
    bottom = jnp.concatenate([blocks, jnp.ones((R, R), jnp.float32)], axis=1)
    return jnp.concatenate([top, middle, bottom], axis=0)


def reference(hamiltonian, margin, pattern, shift_real, shift_imag, residue):
    mask = build_mask(pattern)

    def one_pole(total, inputs):
        real_shift, imag_shift, weight = inputs
        real = (hamiltonian - real_shift * margin) * mask
        imag = (-imag_shift * margin) * mask

        def block(row_lo, row_hi, col_lo, col_hi):
            return real[row_lo:row_hi, col_lo:col_hi], imag[row_lo:row_hi, col_lo:col_hi]

        schur = block(2 * C, N, 2 * C, N)
        inverses, factors = [], []
        for child in range(2):
            low = child * C
            high = low + C
            inverse = newton(block(low, high, low, high))
            factor = cdot(block(2 * C, N, low, high), inverse)
            term = cdot(factor, block(low, high, 2 * C, N))
            schur = (schur[0] - term[0], schur[1] - term[1])
            inverses.append(inverse)
            factors.append(factor)
        root_inv = newton(schur)
        sides, panels, diags = [], [], []
        for child in range(2):
            panel = cdot(root_inv, factors[child])
            panel = (-panel[0], -panel[1])
            side = (panel[0].T, panel[1].T)
            corr = cdot(side, factors[child])
            diag_block = (inverses[child][0] - corr[0], inverses[child][1] - corr[1])
            sides.append(side)
            panels.append(panel)
            diags.append(diag_block)

        def weigh(pair):
            return weight[0] * pair[0] - weight[1] * pair[1]

        empty = jnp.zeros((C, C), jnp.float32)
        first = jnp.concatenate([weigh(diags[0]), empty, weigh(sides[0])], axis=1)
        second = jnp.concatenate([empty, weigh(diags[1]), weigh(sides[1])], axis=1)
        third = jnp.concatenate([weigh(panels[0]), weigh(panels[1]), weigh(root_inv)], axis=1)
        return total + jnp.concatenate([first, second, third], axis=0), None

    start = jnp.zeros((N, N), jnp.float32)
    total, unused = lax.scan(one_pole, start, (shift_real, shift_imag, residue))
    return total * mask
```

```python
import jax
import jax.numpy as jnp
from jax import lax
from jax.sharding import PartitionSpec as P

PREC = lax.Precision.HIGH


def mm(form, a, b):
    return jnp.einsum(form, a, b, precision=PREC, preferred_element_type=jnp.float32)


def cmm(form, a, b):
    return (
        mm(form, a[0], b[0]) - mm(form, a[1], b[1]),
        mm(form, a[0], b[1]) + mm(form, a[1], b[0]),
    )


def cmul(a, b):
    return (a[0] * b[0] - a[1] * b[1], a[0] * b[1] + a[1] * b[0])


def both(fn, pair):
    return (fn(pair[0]), fn(pair[1]))


def split_diag(mat):
    size = mat[0].shape[0]
    eye = jnp.eye(size, dtype=jnp.bool_)
    diag = both(lambda v: jnp.sum(jnp.where(eye, v, 0.0), axis=0), mat)
    denom = diag[0] * diag[0] + diag[1] * diag[1]
    inv = (diag[0] / denom, -diag[1] / denom)
    off = both(lambda v: jnp.where(eye, 0.0, v), mat)
    return inv, off


def build(mesh):
    poles, ng = mesh.shape["pole"], mesh.shape["grid"]
    half, zs = poles // 2, ng // 2
    chips = half * zs
    axes = ("pole", "grid")

    def lin(h, t, c):
        a, r = divmod(t, zs)
        b = zs - 1 - r if a % 2 else r
        return (h * half + a) * ng + 2 * b + c

    every = [(h, t, c) for h in range(2) for t in range(chips) for c in range(2)]
    plus = [(lin(h, t, c), lin(h, (t + 1) % chips, c)) for h, t, c in every]
    minus = [(lin(h, t, c), lin(h, (t - 1) % chips, c)) for h, t, c in every]
    flip = [(lin(h, t, c), lin(1 - h, t, c)) for h, t, c in every]
    swap = [(lin(h, t, c), lin(h, t, 1 - c)) for h, t, c in every]

    def send(x, perm):
        return lax.ppermute(x, axes, perm)

    def local(ham, mar, pattern, shift_real, shift_imag, residue):
        rows, width = ham.shape
        nr, nk = pattern.shape
        sup = width // (nr + nk)
        cc, rr = nk // 2 * sup, nr * sup
        pole, grid = lax.axis_index("pole"), lax.axis_index("grid")
        h, a = pole // half, pole % half
        b, core = grid // 2, grid % 2
        pos = a * zs + jnp.where(a % 2 == 0, b, zs - 1 - b)
        child = a // (half // 2)
        upper = h == 0
        first = core == 0

        def chip_at(t):
            t = t % chips
            ca, r = t // zs, t % zs
            return ca * zs + jnp.where(ca % 2 == 0, r, zs - 1 - r)

        hs = jnp.stack([ham, mar])
        start = jnp.where(upper, cc * child, 2 * cc)
        msg_a = lax.dynamic_slice_in_dim(hs, start, cc, 2)
        wide = hs[:, :, 2 * cc :]
        wide_other = send(wide, flip)
        msg_b = jnp.where(upper, wide, wide_other)
        msg_c = jnp.where(upper, wide_other, wide)[:, :, cc:]

        def ring(msg, extra=None):
            buf = jnp.zeros((chips,) + msg.shape, jnp.float32)
            other = None
            if extra is not None:
                other = jnp.zeros((chips,) + msg.shape, jnp.float32)
            mid = rows // 2

            def put(piece, t, row):
                nonlocal buf, other
                where = (chip_at(t), 0, row, 0)
                buf = lax.dynamic_update_slice(buf, piece[None], where)
                if extra is not None:
                    other = lax.dynamic_update_slice(other, send(piece, extra)[None], where)

            put(msg, pos, 0)
            up, down = msg, msg
            for j in range(1, chips // 2):
                up, down = send(up, plus), send(down, minus)
                put(up, pos - j, 0)
                put(down, pos + j, 0)
            j = chips // 2
            put(send(up[:, :mid], plus), pos - j, 0)
            put(send(down[:, mid:], minus), pos + j, mid)
            return buf if extra is None else (buf, other)

        own_a, got_a = ring(msg_a, flip)
        buf_b = ring(msg_b)
        buf_c = ring(msg_c)
        buf_a = jnp.where(upper, own_a, got_a)
        buf_d = jnp.where(upper, got_a, own_a)

        def gather_core(buf):
            parts = buf.reshape((2, chips // 2) + buf.shape[1:])
            own = lax.dynamic_index_in_dim(parts, core, 0, keepdims=False)
            got = send(lax.dynamic_index_in_dim(parts, 1 - core, 0, keepdims=False), swap)
            lo, hi = jnp.where(first, own, got), jnp.where(first, got, own)
            full = jnp.stack([lo, hi], axis=2)
            full = jnp.swapaxes(full, 0, 1)
            return full.reshape(2, chips * rows, buf.shape[-1])

        def order(own, got, axis=0):
            return jnp.concatenate(
                [jnp.where(first, own, got), jnp.where(first, got, own)], axis=axis
            )

        def shifted(pair, mask=None):
            re, im = pair[0] - shift_real[0] * pair[1], -shift_imag[0] * pair[1]
            return (re, im) if mask is None else (re * mask, im * mask)

        pat = pattern.astype(jnp.float32)
        kid_pat = lax.dynamic_slice_in_dim(pat, core * (nk // 2), nk // 2, 1).T
        kid_mask = jnp.repeat(jnp.repeat(kid_pat, sup, axis=0), sup, axis=1)
        mat_a = shifted(gather_core(buf_a))
        mat_bt = shifted(gather_core(buf_b), kid_mask)
        mat_0 = shifted(jnp.concatenate([gather_core(buf_d), gather_core(buf_c)], axis=2))

        inv, off = split_diag(mat_a)
        row = lambda v: both(lambda w: w[:, None], v)
        col = lambda v: both(lambda w: w[None, :], v)
        scaled = cmul(row(inv), off)
        quad = cmm("ak,kc->ac", off, scaled)
        cube = cmm("ak,kc->ac", quad, scaled)
        inner = tuple(o - q + t for o, q, t in zip(off, quad, cube))
        inner = cmul(cmul(row(inv), inner), col(inv))
        eye = jnp.eye(cc, dtype=jnp.bool_)
        kid_inv = tuple(jnp.where(eye, i[None, :], 0.0) - v for i, v in zip(inv, inner))
        fac_t = cmm("ak,kr->ar", kid_inv, mat_bt)

        rh = rr // 2
        far = both(lambda v: lax.dynamic_slice_in_dim(v, (1 - core) * rh, rh, 1), mat_bt)
        near = both(lambda v: lax.dynamic_slice_in_dim(v, core * rh, rh, 1), mat_bt)
        term_far = both(lambda v: send(v, swap), cmm("cr,cs->rs", far, fac_t))
        fac_other = both(lambda v: send(v, swap), fac_t)
        term_near = cmm("cr,cs->rs", near, fac_t)
        schur_own = tuple(m - u - v for m, u, v in zip(mat_0, term_near, term_far))
        schur = both(lambda v: order(v, send(v, swap)), schur_own)
        full_t = tuple(order(v, w) for v, w in zip(fac_t, fac_other))

        def take(v, blocks, at):
            cut = v.reshape(blocks, ng, rows, v.shape[-1])
            return lax.dynamic_index_in_dim(cut, at, 1, keepdims=False).reshape(
                blocks * rows, v.shape[-1]
            )

        kid_own = both(lambda v: take(v, half // 2, grid), kid_inv)
        kid_got = both(lambda v: send(take(v, half // 2, grid + 1 - 2 * core), swap), kid_inv)
        kid_rows = tuple(order(v, w) for v, w in zip(kid_own, kid_got))

        inv0, off0 = split_diag(schur)
        right = lambda v: cmul(v, col(inv0))
        root_rows = both(lambda v: take(v, half, grid), off0)
        fac_rows = both(lambda v: take(v, half, grid), full_t)
        count = half * rows
        base = right(fac_rows)
        one = cmm("ak,kc->ac", base, off0)
        stacked = tuple(jnp.concatenate([u, v]) for u, v in zip(right(one), right(root_rows)))
        two = cmm("ak,kc->ac", stacked, off0)
        three = cmm("ak,kc->ac", right(two), off0)
        side = tuple(
            v[:count] - u for u, v in zip(base, right(tuple(
                x - y[:count] + z[:count] for x, y, z in zip(one, two, three)
            )))
        )
        spot = (
            jnp.arange(half)[:, None] * ng * rows + grid * rows + jnp.arange(rows)[None, :]
        ).reshape(count)
        hot = spot[:, None] == jnp.arange(rr)[None, :]
        inner0 = right(tuple(x - y[count:] + z[count:] for x, y, z in zip(root_rows, two, three)))
        inner0 = tuple(jnp.where(hot, 1.0 - v if n == 0 else -v, -v) for n, v in enumerate(inner0))
        inv_rows = both(lambda v: take(v[:, None], half, grid), inv0)
        root_inv = cmul(inv_rows, inner0)
        weight_real, weight_imag = residue[0, 0], residue[0, 1]

        def weigh(v):
            return weight_real * v[0] - weight_imag * v[1]

        def reduce(blocks):
            total = lax.dynamic_index_in_dim(blocks, pole, 0, keepdims=False)
            for s in range(1, poles):
                perm = [(p * ng + g, (p ^ s) * ng + g) for p in range(poles) for g in range(ng)]
                total = total + send(
                    lax.dynamic_index_in_dim(blocks, pole ^ s, 0, keepdims=False), perm
                )
            return total

        right_part = jnp.concatenate([weigh(side), weigh(root_inv)]).reshape(poles, rows, rr)
        right_sum = reduce(right_part)
        panel = cmm("ar,cr->ac", root_inv, full_t)
        kc = count // 2
        corr = [
            cmm("ar,cr->ac", both(lambda v: v[k * kc : (k + 1) * kc], side),
                both(lambda v: v[k * cc : (k + 1) * cc], full_t))
            for k in range(2)
        ]
        diag = [
            weigh(tuple(x[k * kc : (k + 1) * kc] - y for x, y in zip(kid_rows, corr[k])))
            for k in range(2)
        ]
        empty = jnp.zeros((kc, cc), jnp.float32)
        left_part = jnp.concatenate(
            [
                jnp.concatenate([diag[0], empty], axis=1),
                jnp.concatenate([empty, diag[1]], axis=1),
                -weigh(panel),
            ]
        ).reshape(poles, rows, 2 * cc)
        left_sum = reduce(left_part)

        ones = jnp.ones((nk // 2, nk // 2), jnp.float32)
        zero = jnp.zeros((nk // 2, nk // 2), jnp.float32)
        table = jnp.concatenate(
            [
                jnp.concatenate([ones, zero, pat[:, : nk // 2].T], axis=1),
                jnp.concatenate([zero, ones, pat[:, nk // 2 :].T], axis=1),
                jnp.concatenate([pat, jnp.ones((nr, nr), jnp.float32)], axis=1),
            ]
        )
        at = (pole * ng + grid) * rows // sup
        line = jnp.repeat(lax.dynamic_index_in_dim(table, at, 0, keepdims=False), sup)
        return jnp.concatenate([left_sum, right_sum], axis=1) * line[None, :]

    return local


def solution(mesh):
    return jax.shard_map(
        build(mesh),
        mesh=mesh,
        in_specs=(
            P(("pole", "grid"), None),
            P(("pole", "grid"), None),
            P(),
            P("pole"),
            P("pole"),
            P("pole", None),
        ),
        out_specs=P(("pole", "grid"), None),
        check_vma=False,
    )
```

```python
import jax
import jax.numpy as jnp
from jax import lax
from jax.experimental import pallas as pl
from jax.experimental.pallas import tpu as pltpu
from jax.sharding import PartitionSpec as P

F32, BF16 = jnp.float32, jnp.bfloat16
NN = (((1,), (0,)), ((), ()))
NT = (((1,), (1,)), ((), ()))
TN = (((0,), (0,)), ((), ()))


def halves(x):
    hi = x.astype(BF16)
    return hi, (x - hi.astype(F32)).astype(BF16)


def store(refs, at, x):
    hi, lo = halves(x)
    refs[0][at] = hi
    refs[1][at] = lo


def dot3(a, b, dims=NN):
    def one(x, y):
        return lax.dot_general(x, y, dims, preferred_element_type=F32)

    return one(a[0], b[0]) + (one(a[0], b[1]) + one(a[1], b[0]))


def triple(refs):
    return [refs[0:2], refs[2:4], refs[4:6]]


def call(kernel, outs, args, scratch, flops, name, limit=40):
    specs = [
        pl.BlockSpec(memory_space=pltpu.SMEM if a.ndim == 1 else pltpu.VMEM) for a in args
    ]
    size = sum(4 * a.size for a in args) + sum(4 * o[0] * o[1] for o in outs)
    return pl.pallas_call(
        kernel,
        out_shape=[jax.ShapeDtypeStruct(o, F32) for o in outs],
        in_specs=specs,
        out_specs=[pl.BlockSpec(memory_space=pltpu.VMEM) for _ in outs],
        scratch_shapes=scratch,
        compiler_params=pltpu.CompilerParams(vmem_limit_bytes=limit << 20),
        cost_estimate=pl.CostEstimate(flops=flops, bytes_accessed=size, transcendentals=0),
        name=name,
    )(*args)


def inverse(re, im):
    denom = re * re + im * im
    return re / denom, -im / denom


def eye_of(rows, cols, shift=0):
    row = lax.broadcasted_iota(jnp.int32, (rows, cols), 0)
    return lax.broadcasted_iota(jnp.int32, (rows, cols), 1) == row + shift


def bf16_pair(rows, cols, count):
    return [pltpu.VMEM((rows, cols), BF16) for _ in range(2 * count)]


TILE = 256


def tiles(width, fn):
    step = min(TILE, width)

    def go(i, _):
        fn(pl.ds(pl.multiple_of(i * step, step), step), i * step)
        return 0

    lax.fori_loop(0, width // step, go, 0)


def left_forms(refs, at, re, im):
    one, two, three = triple(refs)
    store(one, at, re + im)
    store(two, at, re)
    store(three, at, im)


def right_forms(refs, at, re, im):
    one, two, three = triple(refs)
    store(one, at, re)
    store(two, at, im - re)
    store(three, at, re + im)


def gauss(lefts, rights, la, ra, dims=NN):
    k1, k2, k3 = (
        dot3((l[0][la], l[1][la]), (r[0][ra], r[1][ra]), dims)
        for l, r in zip(triple(lefts), triple(rights))
    )
    return k1 - k3, k1 + k2


def kid_kernel(ar, ai, xr, xi, hr, hi, *scratch):
    weights, lefts = scratch[:6], scratch[6:]
    n = ar.shape[0]
    eye = eye_of(n, n)
    re, im = ar[...], ai[...]
    zero = jnp.zeros((), F32)

    def diag(v, axis):
        return jnp.sum(jnp.where(eye, v, zero), axis=axis, keepdims=True)

    cr, ci = inverse(diag(re, 1), diag(im, 1))
    rr, ri = inverse(diag(re, 0), diag(im, 0))
    re, im = jnp.where(eye, zero, re), jnp.where(eye, zero, im)
    wr, wi = cr * re - ci * im, cr * im + ci * re
    right_forms(weights, ..., wr, wi)
    hr[...] = jnp.where(eye, 1.0, -wr)
    hi[...] = -wi
    for _ in range(2):
        left_forms(lefts, ..., hr[...], hi[...])

        def tile(at, start):
            pr, pi = gauss(lefts, weights, ..., (slice(None), at))
            hr[:, at] = jnp.where(eye_of(n, pr.shape[1], -start), 1.0, zero) - pr
            hi[:, at] = -pi

        tiles(n, tile)
    re, im = hr[...], hi[...]
    xr[...] = re * rr - im * ri
    xi[...] = re * ri + im * rr


def kid_inverse(mat):
    n = mat[0].shape[0]
    return call(
        kid_kernel, [(n, n)] * 2, mat,
        [pltpu.VMEM((n, n), F32)] * 2 + bf16_pair(n, n, 6), 12 * n**3, "kid_inverse",
    )


def factor_kernel(xr, xi, br, bi, lr, li, *scratch):
    lefts, one, two, three = scratch[:6], scratch[6:8], scratch[8:10], scratch[10:12]
    re, im = xr[...], xi[...]
    for pair, v in zip(triple(lefts), (re, im - re, re + im)):
        store(pair, ..., v)

    def tile(at, start):
        cols = (slice(None), at)
        c, d = br[cols], bi[cols]
        rights = [halves(c + d), halves(c), halves(d)]
        k1, k2, k3 = (
            dot3((l[0][...], l[1][...]), r) for l, r in zip(triple(lefts), rights)
        )
        lr[cols] = k1 - k3
        li[cols] = k1 + k2

    tiles(br.shape[1], tile)


def factor(x, bt):
    n, m = bt[0].shape
    return call(
        factor_kernel, [(n, m)] * 2, [*x, *bt],
        bf16_pair(n, n, 3) + bf16_pair(n, TILE, 3), 6 * n * n * m, "factor",
    )


def outer_kernel(at_ref, br, bi, lr, li, ur, ui, *scratch):
    lefts, rights = scratch[:6], scratch[6:]
    count = ur.shape[0]
    cols = (slice(None), pl.ds(pl.multiple_of(at_ref[0], TILE), count))
    left_forms(lefts, ..., br[cols].T, bi[cols].T)
    right_forms(rights, ..., lr[...], li[...])

    def tile(at, start):
        pr, pi = gauss(lefts, rights, ..., (slice(None), at))
        ur[:, at] = pr
        ui[:, at] = pi

    tiles(lr.shape[1], tile)


def outer(at, bt, lt, count):
    n, m = bt[0].shape
    return call(
        outer_kernel, [(count, m)] * 2, [at, *bt, *lt],
        bf16_pair(count, n, 3) + bf16_pair(n, m, 3), 6 * n * m * count, "outer",
    )


def root_kernel(blocks, rows, at_ref, w_ref, or_, oi, gr, gi, fr, fi, outr, outi, part, hr, hi,
                rowr, rowi, *scratch):
    weights, lefts = scratch[:6], scratch[6:]
    n = or_.shape[1]
    half = or_.shape[0]
    own = at_ref[0]
    chunk = min(128, half)
    zero = jnp.zeros((), F32)
    square = eye_of(chunk, chunk)
    count = blocks * rows

    for re_ref, im_ref, base in ((or_, oi, own), (gr, gi, half - own)):

        def fill(i, _):
            start = pl.multiple_of(i * chunk, chunk)
            at = pl.multiple_of(base + start, chunk)
            here, there = pl.ds(start, chunk), pl.ds(at, chunk)
            tr, ti = re_ref[here, there], im_ref[here, there]

            def diag(v, axis):
                return jnp.sum(jnp.where(square, v, zero), axis=axis, keepdims=True)

            cr, ci = inverse(diag(tr, 1), diag(ti, 1))
            rr, ri = inverse(diag(tr, 0), diag(ti, 0))
            rowr[:, there] = rr
            rowi[:, there] = ri
            re, im = re_ref[here, :], im_ref[here, :]
            right_forms(weights, (there, slice(None)), cr * re - ci * im, cr * im + ci * re)
            tr, ti = jnp.where(square, zero, tr), jnp.where(square, zero, ti)
            right_forms(weights, (there, there), cr * tr - ci * ti, cr * ti + ci * tr)
            return 0

        lax.fori_loop(0, half // chunk, fill, 0)

    first = at_ref[1]
    for k in range(blocks):
        at = k * (n // blocks) + first
        dst = pl.ds(count + k * rows, rows)
        unit = eye_of(rows, n, at)

        def emit(re_ref, im_ref, start):
            here = pl.ds(pl.multiple_of(at - start, rows), rows)
            re, im = re_ref[here, :], im_ref[here, :]

            def diag(v):
                return jnp.sum(jnp.where(unit, v, zero), axis=1, keepdims=True)

            cr, ci = inverse(diag(re), diag(im))
            wr, wi = cr * re - ci * im, cr * im + ci * re
            hr[dst, :] = jnp.where(unit, 1.0, -wr)
            hi[dst, :] = jnp.where(unit, zero, -wi)

        inside = (at >= own) & (at < own + half)

        @pl.when(inside)
        def _():
            emit(or_, oi, own)

        @pl.when(jnp.logical_not(inside))
        def _():
            emit(gr, gi, half - own)

    def unit_tile(k, width, start):
        return jnp.where(eye_of(rows, width, k * (n // blocks) + first - start), 1.0, zero)

    kid, all_rows = (pl.ds(0, count), slice(None)), (slice(None), slice(None))
    for step in range(3):
        if step == 0:
            left_forms(lefts, kid, fr[...], fi[...])
        else:
            left_forms(lefts, all_rows, hr[...], hi[...])
        span = kid if step == 0 else all_rows

        def tile(at, start):
            pr, pi = gauss(lefts, weights, span, (slice(None), at))
            width = pr.shape[1]
            re, im = fr[:, at] - pr[:count], fi[:, at] - pi[:count]
            if step > 0:
                units = jnp.concatenate([unit_tile(k, width, start) for k in range(blocks)])
                re = jnp.concatenate([re, units - pr[count:]])
                im = jnp.concatenate([im, -pi[count:]])
            if step < 2:
                put = kid[0] if step == 0 else slice(None)
                hr[put, at] = re
                hi[put, at] = im
            else:
                rr, ri = rowr[:, at], rowi[:, at]
                re, im = re * rr - im * ri, re * ri + im * rr
                re = jnp.concatenate([-re[:count], re[count:]])
                im = jnp.concatenate([-im[:count], im[count:]])
                outr[:, at] = re
                outi[:, at] = im
                part[:, at] = w_ref[0] * re - w_ref[1] * im

        tiles(n, tile)


def root(own_at, first, weight, own, got, kid_rows, blocks, rows):
    half, n = own[0].shape
    count = blocks * rows
    at = jnp.stack([own_at, first]).astype(jnp.int32)

    def kernel(*refs):
        root_kernel(blocks, rows, *refs)

    return call(
        kernel, [(2 * count, n)] * 3, [at, weight, *own, *got, *kid_rows],
        [pltpu.VMEM((2 * count, n), F32)] * 2 + [pltpu.VMEM((1, n), F32)] * 2
        + bf16_pair(n, n, 3) + bf16_pair(2 * count, n, 3),
        30 * count * n * n, "root", 48,
    )


def panel_kernel(at_ref, w_ref, gr, gi, x0r, x0i, x1r, x1i, ar, ai, br, bi, out, *scratch):
    re_l, im_l = scratch[0:2], scratch[2:4]
    count = gr.shape[0] // 2
    kc, cc = count // 2, ar.shape[0]
    wr, wi = w_ref[0], w_ref[1]
    re, im = gr[...], gi[...]
    store(re_l, ..., wr * re - wi * im)
    store(im_l, ..., -(wr * im + wi * re))
    out[:count, :] = jnp.zeros((count, out.shape[1]), F32)
    own = at_ref[0]
    for src_r, src_i, kid in ((ar, ai, own), (br, bi, 1 - own)):

        def tile(i, _):
            step = TILE
            here = pl.ds(pl.multiple_of(i * step, step), step)
            at = pl.ds(pl.multiple_of(kid * cc + i * step, step), step)
            c, d = halves(src_r[here, :]), halves(src_i[here, :])

            def product(rows):
                return dot3((re_l[0][rows, :], re_l[1][rows, :]), c, NT) + dot3(
                    (im_l[0][rows, :], im_l[1][rows, :]), d, NT
                )

            out[count:, at] = -product(pl.ds(count, count))
            mine = pl.ds(pl.multiple_of(kid * kc, kc), kc)
            out[mine, at] = -product(mine)
            return 0

        lax.fori_loop(0, cc // TILE, tile, 0)
    for k, (xr, xi) in enumerate(((x0r, x0i), (x1r, x1i))):
        spot = (pl.ds(k * kc, kc), pl.ds(k * cc, cc))
        out[spot] = out[spot] + (wr * xr[...] - wi * xi[...])


def panel(core, weight, pair, kid_rows, own_t, got_t):
    count2, n = pair[0].shape
    cc = own_t[0].shape[0]
    at = core.astype(jnp.int32).reshape(1)
    return call(
        panel_kernel, [(count2, 2 * cc)],
        [at, weight, *pair, *kid_rows[0], *kid_rows[1], *own_t, *got_t],
        bf16_pair(count2, n, 2), 3 * count2 * n * 2 * cc, "panel",
    )[0]


def both(fn, pair):
    return (fn(pair[0]), fn(pair[1]))


def build(mesh):
    poles, ng = mesh.shape["pole"], mesh.shape["grid"]
    half, zs = poles // 2, ng // 2
    chips = half * zs
    axes = ("pole", "grid")

    def lin(h, t, c):
        a, r = divmod(t, zs)
        b = zs - 1 - r if a % 2 else r
        return (h * half + a) * ng + 2 * b + c

    every = [(h, t, c) for h in range(2) for t in range(chips) for c in range(2)]
    plus = [(lin(h, t, c), lin(h, (t + 1) % chips, c)) for h, t, c in every]
    minus = [(lin(h, t, c), lin(h, (t - 1) % chips, c)) for h, t, c in every]
    flip = [(lin(h, t, c), lin(1 - h, t, c)) for h, t, c in every]
    swap = [(lin(h, t, c), lin(h, t, 1 - c)) for h, t, c in every]

    def send(x, perm):
        return lax.ppermute(x, axes, perm)

    def local(ham, mar, pattern, shift_real, shift_imag, residue):
        rows, width = ham.shape
        nr, nk = pattern.shape
        sup = width // (nr + nk)
        cc, rr = nk // 2 * sup, nr * sup
        pole, grid = lax.axis_index("pole"), lax.axis_index("grid")
        h, a = pole // half, pole % half
        b, core = grid // 2, grid % 2
        pos = a * zs + jnp.where(a % 2 == 0, b, zs - 1 - b)
        child = a // (half // 2)
        upper = h == 0
        first = core == 0

        def chip_at(t):
            t = t % chips
            ca, r = t // zs, t % zs
            return ca * zs + jnp.where(ca % 2 == 0, r, zs - 1 - r)

        hs = jnp.stack([ham, mar])
        start = jnp.where(upper, cc * child, 2 * cc)
        msg_a = lax.dynamic_slice_in_dim(hs, start, cc, 2)
        wide = hs[:, :, 2 * cc :]
        wide_other = send(wide, flip)
        msg_b = jnp.where(upper, wide, wide_other)
        msg_c = jnp.where(upper, wide_other, wide)[:, :, cc:]

        def ring(msg, extra=None):
            buf = jnp.zeros((chips,) + msg.shape, jnp.float32)
            other = None
            if extra is not None:
                other = jnp.zeros((chips,) + msg.shape, jnp.float32)
            mid = rows // 2

            def put(piece, t, row):
                nonlocal buf, other
                where = (chip_at(t), 0, row, 0)
                buf = lax.dynamic_update_slice(buf, piece[None], where)
                if extra is not None:
                    other = lax.dynamic_update_slice(other, send(piece, extra)[None], where)

            put(msg, pos, 0)
            up, down = msg, msg
            for j in range(1, chips // 2):
                up, down = send(up, plus), send(down, minus)
                put(up, pos - j, 0)
                put(down, pos + j, 0)
            j = chips // 2
            put(send(up[:, :mid], plus), pos - j, 0)
            put(send(down[:, mid:], minus), pos + j, mid)
            return buf if extra is None else (buf, other)

        own_a, got_a = ring(msg_a, flip)
        buf_b = ring(msg_b)
        buf_c = ring(msg_c)
        buf_a = jnp.where(upper, own_a, got_a)
        buf_d = jnp.where(upper, got_a, own_a)

        def gather_core(buf):
            parts = buf.reshape((2, chips // 2) + buf.shape[1:])
            own = lax.dynamic_index_in_dim(parts, core, 0, keepdims=False)
            got = send(lax.dynamic_index_in_dim(parts, 1 - core, 0, keepdims=False), swap)
            lo, hi = jnp.where(first, own, got), jnp.where(first, got, own)
            full = jnp.stack([lo, hi], axis=2)
            full = jnp.swapaxes(full, 0, 1)
            return full.reshape(2, chips * rows, buf.shape[-1])

        def order(own, got, axis=0):
            return jnp.concatenate(
                [jnp.where(first, own, got), jnp.where(first, got, own)], axis=axis
            )

        def shifted(pair, mask=None):
            re, im = pair[0] - shift_real[0] * pair[1], -shift_imag[0] * pair[1]
            return (re, im) if mask is None else (re * mask, im * mask)

        pat = pattern.astype(jnp.float32)
        kid_pat = lax.dynamic_slice_in_dim(pat, core * (nk // 2), nk // 2, 1).T
        kid_mask = jnp.repeat(jnp.repeat(kid_pat, sup, axis=0), sup, axis=1)
        mat_a = shifted(gather_core(buf_a))
        mat_bt = shifted(gather_core(buf_b), kid_mask)
        mat_0 = shifted(jnp.concatenate([gather_core(buf_d), gather_core(buf_c)], axis=2))

        kid_inv = kid_inverse(mat_a)
        fac_t = factor(kid_inv, mat_bt)
        rh = rr // 2
        own_at, far_at = core * rh, (1 - core) * rh

        def spot(v):
            return v.astype(jnp.int32).reshape(1)

        term_far = both(lambda v: send(v, swap), outer(spot(far_at), mat_bt, fac_t, rh))
        fac_other = both(lambda v: send(v, swap), fac_t)
        term_near = outer(spot(own_at), mat_bt, fac_t, rh)
        schur_own = tuple(m - u - v for m, u, v in zip(mat_0, term_near, term_far))
        schur_got = both(lambda v: send(v, swap), schur_own)

        def take(v, blocks, at):
            cut = v.reshape(blocks, ng, rows, v.shape[-1])
            return lax.dynamic_index_in_dim(cut, at, 1, keepdims=False).reshape(
                blocks * rows, v.shape[-1]
            )

        kid_own = both(lambda v: take(v, half // 2, grid), kid_inv)
        kid_got = both(lambda v: send(take(v, half // 2, grid + 1 - 2 * core), swap), kid_inv)
        lo = tuple(jnp.where(first, v, w) for v, w in zip(kid_own, kid_got))
        hi = tuple(jnp.where(first, w, v) for v, w in zip(kid_own, kid_got))
        fac_own = both(lambda v: take(v, half // 2, grid), fac_t)
        fac_got = both(lambda v: take(v, half // 2, grid), fac_other)
        fac_rows = tuple(order(v, w) for v, w in zip(fac_own, fac_got))

        def reduce(blocks):
            total = lax.dynamic_index_in_dim(blocks, pole, 0, keepdims=False)
            for s in range(1, poles):
                perm = [(p * ng + g, (p ^ s) * ng + g) for p in range(poles) for g in range(ng)]
                total = total + send(
                    lax.dynamic_index_in_dim(blocks, pole ^ s, 0, keepdims=False), perm
                )
            return total

        weight = residue[0]
        *inner, right_part = root(
            own_at, grid * rows, weight, schur_own, schur_got, fac_rows, half, rows
        )
        right_sum = reduce(right_part.reshape(poles, rows, rr))
        left_part = panel(core, weight, inner, (lo, hi), fac_t, fac_other)
        left_sum = reduce(left_part.reshape(poles, rows, 2 * cc))

        ones = jnp.ones((nk // 2, nk // 2), jnp.float32)
        zero = jnp.zeros((nk // 2, nk // 2), jnp.float32)
        table = jnp.concatenate(
            [
                jnp.concatenate([ones, zero, pat[:, : nk // 2].T], axis=1),
                jnp.concatenate([zero, ones, pat[:, nk // 2 :].T], axis=1),
                jnp.concatenate([pat, jnp.ones((nr, nr), jnp.float32)], axis=1),
            ]
        )
        at = (pole * ng + grid) * rows // sup
        line = jnp.repeat(lax.dynamic_index_in_dim(table, at, 0, keepdims=False), sup)
        return jnp.concatenate([left_sum, right_sum], axis=1) * line[None, :]

    return local


def solution(mesh):
    return jax.shard_map(
        build(mesh),
        mesh=mesh,
        in_specs=(
            P(("pole", "grid"), None),
            P(("pole", "grid"), None),
            P(),
            P("pole"),
            P("pole"),
            P("pole", None),
        ),
        out_specs=P(("pole", "grid"), None),
        check_vma=False,
    )
```

```python
import jax
import jax.numpy as jnp
from jax import lax
from jax.experimental import pallas as pl
from jax.experimental.pallas import tpu as pltpu
from jax.sharding import PartitionSpec as P

F32, BF16 = jnp.float32, jnp.bfloat16
NN = (((1,), (0,)), ((), ()))
NT = (((1,), (1,)), ((), ()))
TN = (((0,), (0,)), ((), ()))


def halves(x):
    hi = x.astype(BF16)
    return hi, (x - hi.astype(F32)).astype(BF16)


def store(refs, at, x):
    hi, lo = halves(x)
    refs[0][at] = hi
    refs[1][at] = lo


def stack(ref, at, size, x):
    hi, lo = halves(x)
    rows = x.shape[0]
    ref[at : at + rows, :] = hi
    ref[at + size : at + size + rows, :] = lo


def dot3(left, size, right, dims=NN):
    def one(x, y):
        return lax.dot_general(x, y, dims, preferred_element_type=F32)

    big = one(left[0 : 2 * size, :], right[0])
    return big[:size] + (big[size:] + one(left[0:size, :], right[1]))


def triple(refs):
    return [refs[0:2], refs[2:4], refs[4:6]]


def call(kernel, outs, args, scratch, flops, name, limit=60):
    spaces = [pltpu.SMEM if a.ndim == 1 else pl.ANY if a.ndim > 2 else pltpu.VMEM for a in args]
    specs = [pl.BlockSpec(memory_space=space) for space in spaces]
    size = sum(4 * a.size for a in args) + sum(4 * o[0] * o[1] for o in outs)
    return pl.pallas_call(
        kernel,
        out_shape=[jax.ShapeDtypeStruct(o, F32) for o in outs],
        in_specs=specs,
        out_specs=[pl.BlockSpec(memory_space=pltpu.VMEM) for _ in outs],
        scratch_shapes=scratch,
        compiler_params=pltpu.CompilerParams(vmem_limit_bytes=limit << 20),
        cost_estimate=pl.CostEstimate(flops=flops, bytes_accessed=size, transcendentals=0),
        name=name,
    )(*args)


def inverse(re, im):
    denom = re * re + im * im
    return re / denom, -im / denom


def eye_of(rows, cols, shift=0):
    row = lax.broadcasted_iota(jnp.int32, (rows, cols), 0)
    return lax.broadcasted_iota(jnp.int32, (rows, cols), 1) == row + shift


def left_refs(rows, cols):
    return [pltpu.VMEM((2 * rows, cols), BF16) for _ in range(3)]


def bf16_pair(rows, cols, count):
    return [pltpu.VMEM((rows, cols), BF16) for _ in range(2 * count)]


TILE = 256


def tiles(width, fn):
    step = min(TILE, width)

    def go(i, _):
        fn(pl.ds(pl.multiple_of(i * step, step), step), i * step)
        return 0

    lax.fori_loop(0, width // step, go, 0)


def left_forms(refs, re, im):
    for ref, v in zip(refs, (re + im, re, im)):
        stack(ref, 0, v.shape[0], v)


def right_forms(refs, at, re, im):
    one, two, three = triple(refs)
    store(one, at, re)
    store(two, at, im - re)
    store(three, at, re + im)


def gauss(lefts, size, rights, at):
    k1, k2, k3 = (
        dot3(l, size, (r[0][:, at], r[1][:, at])) for l, r in zip(lefts, triple(rights))
    )
    return k1 - k3, k1 + k2


class Layout:
    def __init__(self, poles, ng):
        self.ng, self.half, self.zs = ng, poles // 2, ng // 2
        self.chips = self.half * self.zs
        pole, grid = lax.axis_index("pole"), lax.axis_index("grid")
        a, b = lax.rem(pole, self.half), lax.div(grid, 2)
        self.core = lax.rem(grid, 2)
        self.upper = pole < self.half
        self.pos = a * self.zs + jnp.where(lax.rem(a, 2) == 0, b, self.zs - 1 - b)

    def chip_at(self, t):
        t = lax.rem(t + self.chips, self.chips)
        a, r = lax.div(t, self.zs), lax.rem(t, self.zs)
        return a * self.zs + jnp.where(lax.rem(a, 2) == 0, r, self.zs - 1 - r)

    def owners(self):
        sign = 1 - 2 * self.core
        steps = range(1, self.chips // 2 + 1)
        at = [self.pos] + [self.pos - sign * j for j in steps] + [self.pos + sign * j for j in steps]
        each = self.chips // 2
        found = [self.chip_at(t) for t in at]
        return [(lax.div(k, each), lax.rem(k, each)) for k in found]


def pull(layout, jobs, sems):
    owners = layout.owners()
    last = layout.chips // 2
    copies = []
    for refs, buf, taken in jobs:
        for n, (ref, (child, k)) in enumerate(zip(refs, owners)):
            cond = child == layout.core
            if taken is not None:
                cond = cond & taken
            dst = buf.at[k]
            if n == last:
                dst = buf.at[k, layout.core]
            elif n == 2 * last:
                dst = buf.at[k, 1 - layout.core]
            copies.append((cond, pltpu.make_async_copy(ref, dst, sems.at[len(copies)])))
    for cond, copy in copies:
        pl.when(cond)(copy.start)

    def wait():
        for cond, copy in copies:
            pl.when(cond)(copy.wait)

    return wait


def pieces(buf, emit):
    count, _, _, rows, _ = buf.shape
    for k in range(count):
        for c in range(2):
            emit(slice((2 * k + c) * rows, (2 * k + c + 1) * rows), k, buf.at[k, c])


def kid_kernel(shape, shift, *refs):
    layout = Layout(*shape)
    count = layout.chips + 1
    own, other, refs = refs[:count], refs[count : 2 * count], refs[2 * count :]
    xr, xi, ar, ai, hr, hi, buf, sems, *scratch = refs
    weights, lefts = scratch[:6], scratch[6:]
    n = ar.shape[0]
    pull(
        layout,
        [(own, buf, layout.upper), (other, buf, jnp.logical_not(layout.upper))],
        sems,
    )()

    def emit(at, k, ref):
        ar[at, :] = ref[0] - shift[0] * ref[1]
        ai[at, :] = -shift[1] * ref[1]

    pieces(buf, emit)
    eye = eye_of(n, n)
    re, im = ar[...], ai[...]
    zero = jnp.zeros((), F32)

    def diag(v, axis):
        return jnp.sum(jnp.where(eye, v, zero), axis=axis, keepdims=True)

    cr, ci = inverse(diag(re, 1), diag(im, 1))
    rr, ri = inverse(diag(re, 0), diag(im, 0))
    re, im = jnp.where(eye, zero, re), jnp.where(eye, zero, im)
    wr, wi = cr * re - ci * im, cr * im + ci * re
    right_forms(weights, ..., wr, wi)
    hr[...] = jnp.where(eye, 1.0, -wr)
    hi[...] = -wi
    for _ in range(2):
        left_forms(lefts, hr[...], hi[...])

        def tile(at, start):
            pr, pi = gauss(lefts, n, weights, at)
            hr[:, at] = jnp.where(eye_of(n, pr.shape[1], -start), 1.0, zero) - pr
            hi[:, at] = -pi

        tiles(n, tile)
    re, im = hr[...], hi[...]
    xr[...] = re * rr - im * ri
    xi[...] = re * ri + im * rr


def raw(own):
    _, _, rows, width = own[0].shape
    return pltpu.VMEM(((len(own) - 1) // 2, 2, 2, rows, width), F32)


def kid_inverse(shape, shift, own, other):
    n = own[0].shape[-1]

    def kernel(*refs):
        kid_kernel(shape, *refs)

    return call(
        kernel, [(n, n)] * 2, [shift, *own, *other],
        [pltpu.VMEM((n, n), F32)] * 4 + [raw(own), pltpu.SemaphoreType.DMA((2 * len(own),))]
        + bf16_pair(n, n, 3) + left_refs(n, n), 12 * n**3, "kid_inverse", 24,
    )


def outer_rows(at, br, bi, lefts, rights, ur, ui):
    count = ur.shape[0]
    cols = (slice(None), pl.ds(pl.multiple_of(at, TILE), count))
    left_forms(lefts, br[cols].T, bi[cols].T)

    def tile(at, start):
        pr, pi = gauss(lefts, count, rights, at)
        ur[:, at] = pr
        ui[:, at] = pi

    tiles(ur.shape[1], tile)


def factor_kernel(shape, dims, shift, pat, xr, xi, *refs):
    layout = Layout(*shape)
    sup, nk = dims
    count = layout.chips + 1
    own, refs = refs[:count], refs[count:]
    br, bi, lr, li, buf, sems, *lefts = refs
    core = layout.core
    rows = buf.shape[3]
    nr = br.shape[1] // sup
    wait = pull(layout, [(own, buf, None)], sems)

    re, im = xr[...], xi[...]
    n = re.shape[0]
    for ref, v in zip(lefts, (re, im - re, re + im)):
        stack(ref, 0, n, v)

    wait()

    def emit(at, k, ref):
        node = 2 * k * rows // sup
        for j in range(nr):
            mask = pat[j * nk + core * (nk // 2) + node]
            cols = slice(j * sup, (j + 1) * sup)
            re = ref[0, :, cols] - shift[0] * ref[1, :, cols]
            br[at, cols] = re * mask
            bi[at, cols] = -shift[1] * ref[1, :, cols] * mask

    pieces(buf, emit)
    def tile(at, start):
        cols = (slice(None), at)
        c, d = br[cols], bi[cols]
        k1, k2, k3 = (
            dot3(l, n, halves(v)) for l, v in zip(lefts, (c + d, c, d))
        )
        re, im = k1 - k3, k1 + k2
        lr[cols] = re
        li[cols] = im

    tiles(br.shape[1], tile)


def factor(shape, shift, pat, x, own, sup, nk):
    n, m = x[0].shape[0], own[0].shape[-1]

    def kernel(*refs):
        factor_kernel(shape, (sup, nk), *refs)

    return call(
        kernel, [(n, m)] * 4, [shift, pat, *x, *own],
        [raw(own), pltpu.SemaphoreType.DMA((len(own),))] + left_refs(n, n),
        6 * n * n * m, "factor", 60,
    )


def far_kernel(at_ref, br, bi, lr, li, ur, ui, *scratch):
    lefts, rights = scratch[:3], scratch[3:]
    right_forms(rights, ..., lr[...], li[...])
    outer_rows(at_ref[1], br, bi, lefts, rights, ur, ui)


def far_rows(at, bt, lt, count):
    n, m = bt[0].shape
    return call(
        far_kernel, [(count, m)] * 2, [at, *bt, *lt],
        left_refs(count, n) + bf16_pair(n, m, 3), 6 * n * m * count, "far", 60,
    )


def schur_kernel(shape, at_ref, shift, br, bi, lr, li, fr, fi, *refs):
    layout = Layout(*shape)
    count = layout.chips + 1
    own, other, last = (refs[k * count : (k + 1) * count] for k in range(3))
    ur, ui, buf_d, buf_c, sems, *scratch = refs[3 * count :]
    lefts, rights = scratch[:3], scratch[3:]
    wait = pull(
        layout,
        [
            (own, buf_d, jnp.logical_not(layout.upper)),
            (other, buf_d, layout.upper),
            (last, buf_c, None),
        ],
        sems,
    )
    right_forms(rights, ..., lr[...], li[...])
    outer_rows(at_ref[1], br, bi, lefts, rights, ur, ui)
    wait()
    width = buf_d.shape[-1]
    for buf, base in ((buf_d, 0), (buf_c, width)):
        cols = slice(base, base + width)

        def emit(at, k, ref):
            re = ref[0] - shift[0] * ref[1]
            ur[at, cols] = re - ur[at, cols] - fr[at, cols]
            ui[at, cols] = -shift[1] * ref[1] - ui[at, cols] - fi[at, cols]

        pieces(buf, emit)


def schur_rows(shape, at, shift, bt, lt, far, own, other, last):
    n, m = bt[0].shape
    count = far[0].shape[0]

    def kernel(*refs):
        schur_kernel(shape, *refs)

    return call(
        kernel, [(count, m)] * 2, [at, shift, *bt, *lt, *far, *own, *other, *last],
        [raw(own), raw(last), pltpu.SemaphoreType.DMA((3 * len(own),))]
        + left_refs(count, n) + bf16_pair(n, m, 3), 6 * n * m * count, "schur", 60,
    )


def root_kernel(blocks, rows, at_ref, w_ref, or_, oi, gr, gi, fr, fi, outr, outi, part, hr, hi,
                rowr, rowi, *scratch):
    weights, lefts = scratch[:6], scratch[6:]
    n = or_.shape[1]
    half = or_.shape[0]
    own = at_ref[0]
    chunk = min(128, half)
    zero = jnp.zeros((), F32)
    square = eye_of(chunk, chunk)
    count = blocks * rows

    for re_ref, im_ref, base in ((or_, oi, own), (gr, gi, half - own)):

        def fill(i, _):
            start = pl.multiple_of(i * chunk, chunk)
            at = pl.multiple_of(base + start, chunk)
            here, there = pl.ds(start, chunk), pl.ds(at, chunk)
            tr, ti = re_ref[here, there], im_ref[here, there]

            def diag(v, axis):
                return jnp.sum(jnp.where(square, v, zero), axis=axis, keepdims=True)

            cr, ci = inverse(diag(tr, 1), diag(ti, 1))
            rr, ri = inverse(diag(tr, 0), diag(ti, 0))
            rowr[:, there] = rr
            rowi[:, there] = ri
            re, im = re_ref[here, :], im_ref[here, :]
            right_forms(weights, (there, slice(None)), cr * re - ci * im, cr * im + ci * re)
            tr, ti = jnp.where(square, zero, tr), jnp.where(square, zero, ti)
            right_forms(weights, (there, there), cr * tr - ci * ti, cr * ti + ci * tr)
            return 0

        lax.fori_loop(0, half // chunk, fill, 0)

    first = at_ref[1]
    for k in range(blocks):
        at = k * (n // blocks) + first
        dst = pl.ds(count + k * rows, rows)
        unit = eye_of(rows, n, at)

        def emit(re_ref, im_ref, start):
            here = pl.ds(pl.multiple_of(at - start, rows), rows)
            re, im = re_ref[here, :], im_ref[here, :]

            def diag(v):
                return jnp.sum(jnp.where(unit, v, zero), axis=1, keepdims=True)

            cr, ci = inverse(diag(re), diag(im))
            wr, wi = cr * re - ci * im, cr * im + ci * re
            hr[dst, :] = jnp.where(unit, 1.0, -wr)
            hi[dst, :] = jnp.where(unit, zero, -wi)

        inside = (at >= own) & (at < own + half)

        @pl.when(inside)
        def _():
            emit(or_, oi, own)

        @pl.when(jnp.logical_not(inside))
        def _():
            emit(gr, gi, half - own)

    def unit_tile(k, width, start):
        return jnp.where(eye_of(rows, width, k * (n // blocks) + first - start), 1.0, zero)

    for step in range(3):
        if step == 0:
            left_forms(lefts, fr[...], fi[...])
        else:
            left_forms(lefts, hr[...], hi[...])
        size = count if step == 0 else 2 * count

        def tile(at, start):
            pr, pi = gauss(lefts, size, weights, at)
            width = pr.shape[1]
            re, im = fr[:, at] - pr[:count], fi[:, at] - pi[:count]
            if step > 0:
                units = jnp.concatenate([unit_tile(k, width, start) for k in range(blocks)])
                re = jnp.concatenate([re, units - pr[count:]])
                im = jnp.concatenate([im, -pi[count:]])
            if step < 2:
                put = slice(0, size)
                hr[put, at] = re
                hi[put, at] = im
            else:
                rr, ri = rowr[:, at], rowi[:, at]
                re, im = re * rr - im * ri, re * ri + im * rr
                re = jnp.concatenate([-re[:count], re[count:]])
                im = jnp.concatenate([-im[:count], im[count:]])
                outr[:, at] = re
                outi[:, at] = im
                part[:, at] = w_ref[0] * re - w_ref[1] * im

        tiles(n, tile)


def root(own_at, first, weight, own, got, kid_rows, blocks, rows):
    half, n = own[0].shape
    count = blocks * rows
    at = jnp.stack([own_at, first]).astype(jnp.int32)

    def kernel(*refs):
        root_kernel(blocks, rows, *refs)

    return call(
        kernel, [(2 * count, n)] * 3, [at, weight, *own, *got, *kid_rows],
        [pltpu.VMEM((2 * count, n), F32)] * 2 + [pltpu.VMEM((1, n), F32)] * 2
        + bf16_pair(n, n, 3) + left_refs(2 * count, n),
        30 * count * n * n, "root", 48,
    )


def panel_kernel(at_ref, w_ref, gr, gi, x0r, x0i, x1r, x1i, ar, ai, br, bi, out, *scratch):
    re_l, im_l = scratch[0:2], scratch[2:4]
    work = scratch[4]
    count = gr.shape[0] // 2
    kc, cc = count // 2, ar.shape[0]
    size = kc + count
    wr, wi = w_ref[0], w_ref[1]
    own = at_ref[0]
    out[:count, :] = jnp.zeros((count, out.shape[1]), F32)
    for n in range(2):
        kid = own if n == 0 else 1 - own
        for src, dst, rows in (
            (pl.ds(pl.multiple_of(kid * kc, kc), kc), 0, kc), (pl.ds(count, count), kc, count)
        ):
            re, im = gr[src, :], gi[src, :]
            stack(re_l[n], dst, size, -(wr * re - wi * im))
            stack(im_l[n], dst, size, wr * im + wi * re)
    for n, (src_r, src_i) in enumerate(((ar, ai), (br, bi))):
        kid = own if n == 0 else 1 - own

        def tile(i, _):
            step = TILE
            here = pl.ds(pl.multiple_of(i * step, step), step)
            at = pl.ds(pl.multiple_of(kid * cc + i * step, step), step)
            work[...] = dot3(re_l[n], size, halves(src_r[here, :]), NT) + dot3(
                im_l[n], size, halves(src_i[here, :]), NT
            )
            out[count:, at] = work[kc:, :]
            out[pl.ds(pl.multiple_of(kid * kc, kc), kc), at] = work[:kc, :]
            return 0

        lax.fori_loop(0, cc // TILE, tile, 0)
    for k, (xr, xi) in enumerate(((x0r, x0i), (x1r, x1i))):
        spot = (pl.ds(k * kc, kc), pl.ds(k * cc, cc))
        out[spot] = out[spot] + (wr * xr[...] - wi * xi[...])


def panel(core, weight, pair, kid_rows, own_t, got_t):
    count2, n = pair[0].shape
    cc = own_t[0].shape[0]
    at = core.astype(jnp.int32).reshape(1)
    return call(
        panel_kernel, [(count2, 2 * cc)],
        [at, weight, *pair, *kid_rows[0], *kid_rows[1], *own_t, *got_t],
        [pltpu.VMEM((3 * count2 // 2, n), BF16) for _ in range(4)]
        + [pltpu.VMEM((3 * count2 // 4, TILE), F32)],
        3 * count2 * n * 2 * cc, "panel", 24,
    )[0]


def both(fn, pair):
    return (fn(pair[0]), fn(pair[1]))


def build(mesh):
    poles, ng = mesh.shape["pole"], mesh.shape["grid"]
    half, zs = poles // 2, ng // 2
    chips = half * zs
    axes = ("pole", "grid")

    def lin(h, t, c):
        a, r = divmod(t, zs)
        b = zs - 1 - r if a % 2 else r
        return (h * half + a) * ng + 2 * b + c

    every = [(h, t, c) for h in range(2) for t in range(chips) for c in range(2)]
    turn = [(lin(h, t, c), lin(h, (t + 1 - 2 * c) % chips, c)) for h, t, c in every]
    flip = [(lin(h, t, c), lin(1 - h, t, c)) for h, t, c in every]
    swap = [(lin(h, t, c), lin(h, t, 1 - c)) for h, t, c in every]

    def send(x, perm):
        return lax.ppermute(x, axes, perm)

    def local(ham, mar, pattern, shift_real, shift_imag, residue):
        rows, width = ham.shape
        nr, nk = pattern.shape
        sup = width // (nr + nk)
        cc, rr = nk // 2 * sup, nr * sup
        pole, grid = lax.axis_index("pole"), lax.axis_index("grid")
        h, a = pole // half, pole % half
        core = grid % 2
        child = a // (half // 2)
        upper = h == 0
        first = core == 0

        hs = jnp.stack([ham, mar])
        start = jnp.where(upper, cc * child, 2 * cc)
        msg_a = lax.dynamic_slice_in_dim(hs, start, cc, 2)
        wide = hs[:, :, 2 * cc :]
        wide_other = send(wide, flip)
        msg_b = jnp.where(upper, wide, wide_other)
        msg_c = jnp.where(upper, wide_other, wide)[:, :, cc:]

        def pair(x):
            got = send(x, swap)
            return jnp.stack([jnp.where(first, x, got), jnp.where(first, got, x)])

        pat = pattern.astype(jnp.float32)
        rh = rr // 2
        shift = jnp.concatenate([shift_real, shift_imag])
        own_at = core * rh
        near_at = jnp.stack([core, own_at]).astype(jnp.int32)
        far_at = jnp.stack([core, (1 - core) * rh]).astype(jnp.int32)
        shape = (poles, ng)
        last = chips // 2

        def step(got, j):
            if j == last:
                return send(lax.dynamic_index_in_dim(got, core, 0, keepdims=False), turn)
            return send(got, turn)

        def shared(name):
            known = {**val, **new}
            return [known[name, j] for j in range(last + 1)] + [
                known[name + "s", j] for j in range(1, last + 1)
            ]

        val = {("a", 0): pair(msg_a)}
        late = {}
        for r in range(1, 2 * last + 2):
            new, held = {}, late
            late = {}
            if r == 1:
                late["w"] = send(wide, flip)
                late["g"] = send(msg_a, flip)
            if r == 3:
                wide_other, flipped = val["w"], val["g"]
                val["f", 0] = pair(flipped)
                val["b", 0] = pair(jnp.where(upper, wide, wide_other))
                val["c", 0] = pair(jnp.where(upper, wide_other, wide)[:, :, cc:])
            for name, j in (("a", r), ("b", r - 2), ("c", r - last - 1)):
                if 1 <= j <= last:
                    new[name, j] = step(val[name, j - 1], j)
                if 2 <= j <= last + 1:
                    new[name + "s", j - 1] = send(val[name, j - 1], swap)
            for j in range(1, last + 1):
                if r == j + 1:
                    (new if j > 1 else late)["f", j] = send(val["a", j], flip)
                if ("f", j) in val and ("fs", j) not in val:
                    new["fs", j] = send(val["f", j], swap)
            if r == last + 2:
                new["x"] = kid_inverse(shape, shift, shared("a"), shared("f"))
            if r == last + 3:
                new["l"] = factor(shape, shift, pat.reshape(-1), val["x"], shared("b"), sup, nk)
            if r == last + 4:
                new["u"] = far_rows(far_at, val["l"][0:2], val["l"][2:4], rh)
            new.update(held)
            keys = list(new)
            if keys:
                val.update(zip(keys, lax.optimization_barrier([new[k] for k in keys])))
        kid_inv = val["x"]
        parts = val["l"]
        mat_bt, fac_t = parts[0:2], parts[2:4]
        new = {("cs", last): send(val["c", last], swap)}
        own_a, other_a, all_c = shared("a"), shared("f"), shared("c")

        def order(own, got, axis=0):
            return jnp.concatenate(
                [jnp.where(first, own, got), jnp.where(first, got, own)], axis=axis
            )

        term_far = both(lambda v: send(v, swap), val["u"])
        fac_other = both(lambda v: send(v, swap), fac_t)
        schur_own = schur_rows(
            shape, near_at, shift, mat_bt, fac_t, term_far, own_a, other_a, all_c
        )
        schur_got = both(lambda v: send(v, swap), schur_own)

        def take(v, blocks, at):
            cut = v.reshape(blocks, ng, rows, v.shape[-1])
            return lax.dynamic_index_in_dim(cut, at, 1, keepdims=False).reshape(
                blocks * rows, v.shape[-1]
            )

        kid_own = both(lambda v: take(v, half // 2, grid), kid_inv)
        kid_got = both(lambda v: send(take(v, half // 2, grid + 1 - 2 * core), swap), kid_inv)
        lo = tuple(jnp.where(first, v, w) for v, w in zip(kid_own, kid_got))
        hi = tuple(jnp.where(first, w, v) for v, w in zip(kid_own, kid_got))
        fac_own = both(lambda v: take(v, half // 2, grid), fac_t)
        fac_got = both(lambda v: take(v, half // 2, grid), fac_other)
        fac_rows = tuple(order(v, w) for v, w in zip(fac_own, fac_got))

        def reduce(blocks):
            total = lax.dynamic_index_in_dim(blocks, pole, 0, keepdims=False)
            for s in range(1, poles):
                perm = [(p * ng + g, (p ^ s) * ng + g) for p in range(poles) for g in range(ng)]
                total = total + send(
                    lax.dynamic_index_in_dim(blocks, pole ^ s, 0, keepdims=False), perm
                )
            return total

        weight = residue[0]
        *inner, right_part = root(
            own_at, grid * rows, weight, schur_own, schur_got, fac_rows, half, rows
        )
        right_sum = reduce(right_part.reshape(poles, rows, rr))
        left_part = panel(core, weight, inner, (lo, hi), fac_t, fac_other)
        left_sum = reduce(left_part.reshape(poles, rows, 2 * cc))

        ones = jnp.ones((nk // 2, nk // 2), jnp.float32)
        zero = jnp.zeros((nk // 2, nk // 2), jnp.float32)
        table = jnp.concatenate(
            [
                jnp.concatenate([ones, zero, pat[:, : nk // 2].T], axis=1),
                jnp.concatenate([zero, ones, pat[:, nk // 2 :].T], axis=1),
                jnp.concatenate([pat, jnp.ones((nr, nr), jnp.float32)], axis=1),
            ]
        )
        at = (pole * ng + grid) * rows // sup
        line = jnp.repeat(lax.dynamic_index_in_dim(table, at, 0, keepdims=False), sup)
        return jnp.concatenate([left_sum, right_sum], axis=1) * line[None, :]

    return local


def solution(mesh):
    return jax.shard_map(
        build(mesh),
        mesh=mesh,
        in_specs=(
            P(("pole", "grid"), None),
            P(("pole", "grid"), None),
            P(),
            P("pole"),
            P("pole"),
            P("pole", None),
        ),
        out_specs=P(("pole", "grid"), None),
        check_vma=False,
    )
```
